256 devices in a mesh: dp: 16 (over x, y), tensor: 16 (over z, core).
Axes of the slice: x: 4, y: 4, z: 8, core: 2. Of those that a mesh axis runs over, the one named last changes fastest.
Arguments:
- tokens: bfloat16 [8192, 8192], P(('dp', 'tensor')), may hold values from -6 to 6
- w_query: bfloat16 [8192, 8192], P(None, 'tensor'), may hold values from -0.0625 to 0.0625
- cotangent: bfloat16 [8192, 8192], P('dp', 'tensor'), may hold values from -6 to 6
- task_embed: bfloat16 [128, 1024], replicated, may hold values from -6 to 6
- w_hidden: bfloat16 [1024, 512], P(None, 'tensor'), may hold values from -0.1875 to 0.1875
- head_a: bfloat16 [512, 16, 8192], P(None, 'dp', 'tensor'), may hold values from -0.0234375 to 0.0234375
- head_b: bfloat16 [512, 16, 8192], P(None, 'dp', 'tensor'), may hold values from -0.0234375 to 0.0234375
- block_task: int32 [16], replicated, may hold values from 0 to 127
Outputs:
- output: bfloat16 [8192, 8192], P('dp', 'tensor')
- grad_tokens: bfloat16 [8192, 8192], P(('dp', 'tensor'))
- grad_head_a: bfloat16 [512, 16, 8192], P(None, 'dp', 'tensor')
- grad_head_b: bfloat16 [512, 16, 8192], P(None, 'dp', 'tensor')
The draws below stay inside these ranges and needn't reach their ends.
All inputs are finite; a program needn't handle non-finite values.
Results may differ from the reference program's by a relative error of at most 0.0077.
Values may be sent and summed in bfloat16 or wider, within the bound.
No kernel may reach another device: no remote copies, remote signals or barrier semaphores. Data moves between devices by JAX's collectives and lax.ppermute only.
A program may use at most 128 MiB of HBM per device.

```python
import math
import jax
import jax.numpy as jnp
import numpy as np
from jax import lax

MODEL_DIM = 8192
R = 16
HID = 512
EMB = 1024
NTASK = 128
BLOCK_TOKENS = 512
NBLK = 16
TOTAL_TOKENS = 8192


def touch_ends(array, own_key, smallest, top_value):
    longest = array.shape.index(max(array.shape))
    spots = []
    for shift in (0, 1):
        where = [jax.random.randint(jax.random.fold_in(own_key, axis), (), 0, length) for axis, length in enumerate(array.shape)]
        where[longest] = (where[longest] + shift) % array.shape[longest]
        spots.append(tuple(where))
    return array.at[spots[0]].set(smallest).at[spots[1]].set(top_value)


def levels(stream_key, dims, shards, least, largest):
    level, own = 1.0, jax.random.fold_in(stream_key, 6)
    for position, parts in shards:
        draws = jnp.exp(jax.random.uniform(jax.random.fold_in(own, position), (parts,), jnp.float32, least / len(shards), largest / len(shards)))
        level = level * jnp.repeat(draws, dims[position] // parts).reshape([-1 if axis == position else 1 for axis in range(len(dims))])
    return level


def rank_table(count, skew):
    portions = [(1 << 20) // math.isqrt(grade ** skew) + 1 for grade in range(1, count + 1)]
    scale = 1 + sum(portions) // (1 << 30)
    return np.cumsum(np.array([max(1, weight // scale) for weight in portions]))


def ranked_ids(key, dims, count, lean):
    table = rank_table(count, lean)
    pick = jax.random.randint(jax.random.fold_in(key, 1), dims, 0, int(table[count - 1]))
    rank = jnp.searchsorted(jnp.asarray(table, jnp.int32), pick, side="right")
    return jax.random.permutation(jax.random.fold_in(key, 2), count)[rank].astype(jnp.int32)


def normal_values(key, dims, deviation, reach, split=(), kind=jnp.bfloat16):
    result = deviation * jax.random.normal(key, dims, jnp.float32)
    if split:
        result = result * levels(key, dims, split, -0.22, 0.18)
    return jnp.clip(result, -reach, reach).astype(kind)


def setup_inputs(seed: int = 0) -> dict:
    seeds = jax.random.split(jax.random.key(seed), 9)
    tokens = normal_values(seeds[0], (TOTAL_TOKENS, MODEL_DIM), 1.0, 6.0, ((0, 256),))
    w_query = normal_values(seeds[1], (MODEL_DIM, MODEL_DIM), MODEL_DIM ** -0.5, 0.0625, ((1, 16),))
    cotangent = normal_values(seeds[2], (TOTAL_TOKENS, MODEL_DIM), 1.0, 6.0, ((0, 16), (1, 16)))
    task_embed = normal_values(seeds[3], (NTASK, EMB), 1.0, 6.0)
    w_hidden = normal_values(seeds[4], (EMB, HID), EMB ** -0.5, 0.1875, ((1, 16),))
    head_a = normal_values(seeds[5], (HID, R, MODEL_DIM), (HID * 128) ** -0.5, 0.0234375, ((1, 16), (2, 16)))
    head_b = normal_values(seeds[6], (HID, R, MODEL_DIM), (HID * 128) ** -0.5, 0.0234375, ((1, 16), (2, 16)))
    block_task = touch_ends(ranked_ids(seeds[7], (NBLK,), NTASK, 2), jax.random.fold_in(seeds[7], 3), 0, NTASK - 1).astype(jnp.int32)
    return {"tokens": tokens, "w_query": w_query, "cotangent": cotangent, "task_embed": task_embed, "w_hidden": w_hidden, "head_a": head_a, "head_b": head_b, "block_task": block_task}


def reference(tokens, w_query, cotangent, task_embed, w_hidden, head_a, head_b, block_task):
    single_float = jnp.float32
    brain_half_float = jnp.bfloat16
    hidden = jax.nn.silu(jnp.dot(task_embed, w_hidden, preferred_element_type=single_float)).astype(brain_half_float)
    hid_blocks = hidden[block_task]
    adapter_down_weight = jnp.dot(hid_blocks, head_a.reshape(HID, R * MODEL_DIM), preferred_element_type=single_float).astype(brain_half_float).reshape(NBLK, R, MODEL_DIM)
    adapter_up_weight = jnp.dot(hid_blocks, head_b.reshape(HID, R * MODEL_DIM), preferred_element_type=single_float).astype(brain_half_float).reshape(NBLK, R, MODEL_DIM)
    block_inputs = tokens.reshape(NBLK, BLOCK_TOKENS, MODEL_DIM).astype(single_float)
    block_output_grads = cotangent.reshape(NBLK, BLOCK_TOKENS, MODEL_DIM).astype(single_float)
    frozen_output = jnp.dot(tokens, w_query, preferred_element_type=single_float)
    down_projection = jnp.einsum("grs,gps->grp", block_inputs, adapter_down_weight.astype(single_float))
    down_low_rank = down_projection.astype(brain_half_float)
    low_rank_update = jnp.einsum("elm,emn->eln", down_low_rank.astype(single_float), adapter_up_weight.astype(single_float)).reshape(TOTAL_TOKENS, MODEL_DIM)
    output = (frozen_output + low_rank_update).astype(brain_half_float)
    backward_input = jnp.einsum("grs,gps->grp", block_output_grads, adapter_up_weight.astype(single_float))
    backward_low_rank = backward_input.astype(brain_half_float)
    frozen = lax.dot_general(cotangent, w_query, (((1,), (1,)), ((), ())), preferred_element_type=single_float)
    adapter_output = jnp.einsum("elm,emn->eln", backward_low_rank.astype(single_float), adapter_down_weight.astype(single_float)).reshape(TOTAL_TOKENS, MODEL_DIM)
    grad_tokens = (frozen + adapter_output).astype(brain_half_float)
    adapter_down_gradient = (jnp.einsum("evr,evx->erx", backward_low_rank.astype(single_float), block_inputs) / BLOCK_TOKENS).astype(brain_half_float)
    adapter_up_gradient = (jnp.einsum("evr,evx->erx", down_low_rank.astype(single_float), block_output_grads) / BLOCK_TOKENS).astype(brain_half_float)
    hid_f = hid_blocks.astype(single_float)
    grad_head_a = lax.dot_general(hid_f, adapter_down_gradient.astype(single_float).reshape(NBLK, R * MODEL_DIM), (((0,), (0,)), ((), ())), precision=lax.Precision.HIGHEST)
    grad_head_b = lax.dot_general(hid_f, adapter_up_gradient.astype(single_float).reshape(NBLK, R * MODEL_DIM), (((0,), (0,)), ((), ())), precision=lax.Precision.HIGHEST)
    return (output, grad_tokens, grad_head_a.reshape(HID, R, MODEL_DIM).astype(brain_half_float), grad_head_b.reshape(HID, R, MODEL_DIM).astype(brain_half_float))
```

```python
import jax
import jax.numpy as jnp
from jax import lax
from jax.sharding import PartitionSpec as P

F32 = jnp.float32
BF16 = jnp.bfloat16


def dot(a, b, ca, cb):
    return lax.dot_general(a, b, (((ca,), (cb,)), ((), ())), preferred_element_type=F32)


def local(tokens, w_query, cotangent, task_embed, w_hidden, head_a, head_b, block_task):
    shard = lax.axis_index("tensor")
    hid_count, rank_rows, width = head_a.shape
    ntasks = task_embed.shape[0]
    blocks = block_task.shape[0]
    rows = cotangent.shape[0]
    whole = lax.all_gather(tokens, "tensor", axis=0, tiled=True)
    hid_part = jax.nn.silu(dot(task_embed, w_hidden, 1, 0)).astype(BF16)
    pick = (block_task[:, None] == jnp.arange(ntasks, dtype=jnp.int32)[None, :]).astype(BF16)
    hid_part = dot(pick, hid_part, 1, 0).astype(BF16)
    hidden = lax.all_gather(hid_part, "tensor", axis=1, tiled=True)
    gen_a = dot(hidden, head_a.reshape(hid_count, width), 1, 0).astype(BF16)
    gen_b = dot(hidden, head_b.reshape(hid_count, width), 1, 0).astype(BF16)
    factors = lax.all_to_all(jnp.stack([gen_a, gen_b], 1), "dp", 0, 0, tiled=True)
    down_w = factors[:, 0]
    up_w = factors[:, 1]
    rank = down_w.shape[0]
    back_part = dot(up_w, cotangent, 1, 1).astype(BF16)
    both = lax.all_gather(jnp.concatenate([down_w, back_part], 0), "tensor", axis=0, tiled=False)
    back_low = both[:, rank:].astype(F32).sum(0).astype(BF16)
    full_a = both[:, :rank].transpose(1, 0, 2).reshape(rank, -1)
    grad_part = (dot(cotangent, w_query, 1, 1) + dot(back_part, full_a, 0, 0)).astype(BF16)
    grad_tokens = lax.psum_scatter(grad_part, "tensor", scatter_dimension=0, tiled=True)
    down_low = dot(whole, full_a, 1, 1).astype(BF16)
    columns = lax.dynamic_slice_in_dim(whole, shard * width, width, 1)
    scale = 1.0 / rows
    grad_a = (dot(back_low, columns, 1, 0) * scale).astype(BF16)
    grad_b = (dot(down_low, cotangent, 0, 0) * scale).astype(BF16)
    own = lax.all_to_all(jnp.stack([grad_a, grad_b], 1), "dp", 0, 0, tiled=True)
    head_grad_a = dot(hidden, own[:, 0], 0, 0).astype(BF16).reshape(hid_count, rank_rows, width)
    head_grad_b = dot(hidden, own[:, 1], 0, 0).astype(BF16).reshape(hid_count, rank_rows, width)
    output = (dot(whole, w_query, 1, 0) + dot(down_low, up_w, 1, 0)).astype(BF16)
    return (output, grad_tokens, head_grad_a, head_grad_b)


def solution(mesh):
    return jax.shard_map(
        local,
        mesh=mesh,
        in_specs=(
            P(("dp", "tensor"), None),
            P(None, "tensor"),
            P("dp", "tensor"),
            P(),
            P(None, "tensor"),
            P(None, "dp", "tensor"),
            P(None, "dp", "tensor"),
            P(),
        ),
        out_specs=(
            P("dp", "tensor"),
            P(("dp", "tensor"), None),
            P(None, "dp", "tensor"),
            P(None, "dp", "tensor"),
        ),
        check_vma=False,
    )
```

```python
import jax
import jax.numpy as jnp
from jax import lax
from jax.sharding import Mesh
from jax.sharding import PartitionSpec as P

F32 = jnp.float32
BF16 = jnp.bfloat16
AXIS = ("z", "core")


def dot(a, b, ca, cb):
    return lax.dot_general(a, b, (((ca,), (cb,)), ((), ())), preferred_element_type=F32)


def gather_small(x):
    n = lax.axis_size(AXIS)
    return lax.all_to_all(jnp.broadcast_to(x[None], (n,) + x.shape), AXIS, 0, 0, tiled=True)


def local(tokens, w_query, cotangent, task_embed, w_hidden, head_a, head_b, block_task):
    shards = lax.axis_size(AXIS)
    chips = shards // 2
    shard = lax.axis_index(AXIS)
    hid_count, rank_rows, width = head_a.shape
    ntasks = task_embed.shape[0]
    rows = cotangent.shape[0]
    part = rows // shards

    whole = lax.all_gather(tokens, AXIS, axis=0, tiled=True)
    hid_part = jax.nn.silu(dot(task_embed, w_hidden, 1, 0)).astype(BF16)
    pick = (block_task[:, None] == jnp.arange(ntasks, dtype=jnp.int32)[None, :]).astype(BF16)
    hid_part = dot(pick, hid_part, 1, 0).astype(BF16)
    hidden = gather_small(hid_part).transpose(1, 0, 2).reshape(hid_part.shape[0], hid_count)
    core = lax.axis_index("core")
    order = jnp.arange(chips * part, dtype=jnp.int32)
    base_row = (order // part) * (2 * part) + order % part
    every = jnp.arange(rows, dtype=jnp.int32)[None, :]
    own_pick = (base_row[:, None] + core * part == every).astype(BF16)
    sib_pick = (base_row[:, None] + (1 - core) * part == every).astype(BF16)
    late_cot, hidden = lax.optimization_barrier((cotangent, hidden))
    cot_own = dot(own_pick, late_cot, 1, 0).astype(BF16)
    cot_sib = dot(sib_pick, late_cot, 1, 0).astype(BF16)
    theirs = dot(cot_sib, w_query, 1, 1).astype(BF16)
    swapped = lax.ppermute(theirs, "core", [(0, 1), (1, 0)])
    mine = (dot(cot_own, w_query, 1, 1) + swapped.astype(F32)).astype(BF16)
    reduced = lax.psum_scatter(mine, "z", scatter_dimension=0, tiled=True)
    gen_a = dot(hidden, head_a.reshape(hid_count, width), 1, 0).astype(BF16)
    gen_b = dot(hidden, head_b.reshape(hid_count, width), 1, 0).astype(BF16)
    factors = lax.all_to_all(jnp.stack([gen_a, gen_b], 1), "dp", 0, 0, tiled=True)
    down_w = factors[:, 0]
    up_w = factors[:, 1]
    rank = down_w.shape[0]
    back_part = dot(up_w, cotangent, 1, 1).astype(BF16)
    both = gather_small(jnp.concatenate([down_w, back_part], 0))
    back_low = both[:, rank:].astype(F32).sum(0).astype(BF16)
    full_a = both[:, :rank].transpose(1, 0, 2).reshape(rank, -1)

    down_low = dot(whole, full_a, 1, 1).astype(BF16)
    columns = lax.dynamic_slice_in_dim(whole, shard * width, width, 1)
    scale = 1.0 / rows
    grad_a = (dot(back_low, columns, 1, 0) * scale).astype(BF16)
    grad_b = (dot(down_low, cotangent, 0, 0) * scale).astype(BF16)
    own = lax.all_to_all(jnp.stack([grad_a, grad_b], 1), "dp", 0, 0, tiled=True)
    head_grad_a = dot(hidden, own[:, 0], 0, 0).astype(BF16).reshape(hid_count, rank_rows, width)
    head_grad_b = dot(hidden, own[:, 1], 0, 0).astype(BF16).reshape(hid_count, rank_rows, width)
    output = (dot(whole, w_query, 1, 0) + dot(down_low, up_w, 1, 0)).astype(BF16)
    back_low, output, head_grad_a, head_grad_b = lax.optimization_barrier(
        (back_low, output, head_grad_a, head_grad_b)
    )
    back_rows = lax.dynamic_slice_in_dim(back_low, shard * part, part, 1)
    grad_tokens = (dot(back_rows, full_a, 0, 0) + reduced.astype(F32)).astype(BF16)
    return (output, grad_tokens, head_grad_a, head_grad_b)


def solution(mesh):
    dp, tensor = mesh.devices.shape
    small = Mesh(mesh.devices.reshape(dp, tensor // 2, 2), ("dp",) + AXIS)
    return jax.shard_map(
        local,
        mesh=small,
        in_specs=(
            P(("dp",) + AXIS, None),
            P(None, AXIS),
            P("dp", AXIS),
            P(),
            P(None, AXIS),
            P(None, "dp", AXIS),
            P(None, "dp", AXIS),
            P(),
        ),
        out_specs=(
            P("dp", AXIS),
            P(("dp",) + AXIS, None),
            P(None, "dp", AXIS),
            P(None, "dp", AXIS),
        ),
        check_vma=False,
    )
```
